32 devices in a mesh: vocab: 4 (over x, core), fsdp: 8 (over z, y).
Axes of the slice: x: 2, y: 2, z: 4, core: 2. Of those that a mesh axis runs over, the one named last changes fastest.
Arguments:
- hidden: bfloat16 [2, 384, 4096], P(None, 'fsdp'), may hold values from -1000 to 1000
- norm_gain: bfloat16 [4096], replicated, may hold values from 0.5 to 1.5
- labels: int32 [2, 384], P(None, 'fsdp'), may hold values from 0 to 65535
- head_weight: bfloat16 [4096, 65536], P(None, ('vocab', 'fsdp')), may hold values from -1 to 1
- head_ema: float32 [4096, 65536], P(None, ('vocab', 'fsdp')), may hold values from 1e-09 to 0.001
- gain_ema: float32 [4096], replicated, may hold values from 0.0001 to 0.03
Outputs:
- head_ema_new: float32 [4096, 65536], P(None, ('vocab', 'fsdp'))
- gain_ema_new: float32 [4096], replicated
The draws below stay inside these ranges and needn't reach their ends.
All inputs are finite; a program needn't handle non-finite values.
Results may differ from the reference program's by a relative error of at most 0.00049.
Values may be sent and summed in bfloat16 or wider, within the bound.
A program may use at most 192 MiB of HBM per device.

```python
import math
import jax
import jax.numpy as jnp
import numpy as np
from jax import lax

D = 4096
V = 65536
MB = 2
TOKENS = 384


def build_pair(key):
    base_key = jax.random.fold_in(key, 7)
    k_weight, k_common, k_noise, k_rows, k_cols = jax.random.split(base_key, 5)
    weight = jax.random.normal(k_weight, (D, V), jnp.float32) * (3.0 / math.sqrt(D))
    noise = jax.random.normal(k_noise, (MB, TOKENS, D), jnp.float32)
    common = jax.random.normal(k_common, (D,), jnp.float32)
    row_scale = jnp.exp(jax.random.uniform(k_rows, (MB, TOKENS, 1), jnp.float32, 0.0, math.log(10.0)))
    col_scale = jnp.exp(jax.random.uniform(k_cols, (D,), jnp.float32, 0.0, math.log(10.0)))
    states = (noise + common[None, None, :]) * row_scale * col_scale[None, None, :]
    limit = 1.0 + 2600 // D
    states = jnp.clip(states, -1000.0, 1000.0)
    weight = jnp.clip(weight, -limit, limit)
    return (states, weight)


def draw_hidden(key, part):
    states, weight = build_pair(key)
    return states.astype(jnp.bfloat16)


def draw_head_weight(key, part):
    states, weight = build_pair(key)
    return weight.astype(jnp.bfloat16)


def set_ends(values, rng, low, largest):
    extent = values.shape
    index_at = [jax.random.randint(jax.random.fold_in(rng, axis), (), 0, extent[axis]) for axis in range(len(extent))]
    values = values.at[tuple(index_at)].set(low)
    longest = extent.index(max(extent))
    index_at[longest] = (index_at[longest] + 1) % extent[longest]
    return values.at[tuple(index_at)].set(largest)


def block_levels(rng, extent, cuts, smallest, top_value):
    level = 1.0
    for position, shards_of in cuts:
        heights = jax.random.uniform(jax.random.fold_in(jax.random.fold_in(rng, 6), position), (shards_of,), jnp.float32, smallest / len(cuts), top_value / len(cuts))
        level = level * jnp.repeat(jnp.exp(heights), extent[position] // shards_of).reshape((-1,) + (1,) * (len(extent) - 1 - position))
    return level


def rank_table(number_of, skew):
    weights = [(1 << 20) // math.isqrt(rank ** skew) + 1 for rank in range(1, number_of + 1)]
    scale = 1 + sum(weights) // (1 << 30)
    return np.cumsum(np.array([max(1, weight // scale) for weight in weights]))


def ranked_ids(own_key, shape, amount, skew):
    grid = rank_table(amount, skew)
    lot = jax.random.randint(jax.random.fold_in(own_key, 1), shape, 0, int(grid[amount - 1]))
    standing = jnp.searchsorted(jnp.asarray(grid, jnp.int32), lot, side="right")
    return jax.random.permutation(jax.random.fold_in(own_key, 2), amount)[standing].astype(jnp.int32)


def setup_inputs(seed: int = 0) -> dict:
    splits = jax.random.split(jax.random.key(seed), 7)
    return {
        "hidden": draw_hidden(jax.random.fold_in(splits[6], 71), 0),
        "norm_gain": jnp.clip(1.0 + 0.1 * jax.random.normal(splits[1], (D,), jnp.float32), 0.5, 1.5).astype(jnp.bfloat16),
        "labels": set_ends(ranked_ids(splits[2], (MB, TOKENS), V, 2), jax.random.fold_in(splits[2], 3), 0, V - 1).astype(jnp.int32),
        "head_weight": draw_head_weight(jax.random.fold_in(splits[6], 71), 0),
        "head_ema": jnp.clip(jnp.exp(math.log(0.001) - 13.815511 * jax.random.uniform(splits[4], (D, V), jnp.float32) ** block_levels(splits[4], (D, V), ((1, 32),), -0.2, 0.2)), 9.999999717180685e-10, 0.001),
        "gain_ema": jnp.clip(jnp.exp(jax.random.uniform(splits[5], (D,), jnp.float32, math.log(0.0001), math.log(0.03))), 0.0001, 0.03),
    }


BETA = 0.99
EPS = 1e-05

def normalize(hidden, norm_gain):
    wide = hidden.astype(jnp.float32)
    factor = lax.rsqrt(lax.optimization_barrier(jnp.mean(wide * wide, axis=-1, keepdims=True)) + EPS)
    return (wide * factor * norm_gain.astype(jnp.float32)).astype(jnp.bfloat16)

def reference(hidden, norm_gain, labels, head_weight, head_ema, gain_ema):
    scaled = normalize(hidden, norm_gain)
    columns = lax.iota(jnp.int32, V)
    gradient = jnp.zeros((D, V), jnp.float32)
    for batch in range(MB):
        logits = jnp.dot(scaled[batch], head_weight, preferred_element_type=jnp.float32)
        row_top = lax.optimization_barrier(jnp.max(logits, axis=1, keepdims=True))
        shifted = jnp.exp(logits - row_top)
        chances = shifted / lax.optimization_barrier(jnp.sum(shifted, axis=1, keepdims=True))
        hits = (labels[batch][:, None] == columns[None, :]).astype(jnp.float32)
        slope = (chances - hits).astype(jnp.bfloat16)
        gradient = gradient + jnp.dot(scaled[batch].T, slope, preferred_element_type=jnp.float32)
    count = MB * TOKENS
    head_new = BETA * head_ema + (1.0 - BETA) * gradient * gradient / count
    gain_grad = lax.optimization_barrier(jnp.sum(head_weight.astype(jnp.float32) * gradient, axis=1)) / norm_gain.astype(jnp.float32)
    gain_new = BETA * gain_ema + (1.0 - BETA) * gain_grad * gain_grad / count
    return (head_new, gain_new)
```

```python
import functools

import jax
import jax.numpy as jnp
from jax import lax
from jax.experimental import pallas as pl
from jax.experimental.pallas import tpu as pltpu
from jax.sharding import PartitionSpec as P

BETA = 0.99
EPS = 1e-05
LANES = 128
PIECES = 4
LAG = 2
MESH = pl.DeviceIdType.MESH
MIB = 1024 * 1024


def forward_kernel(
    parts,
    ways,
    hidden_ref,
    gain_ref,
    label_ref,
    weight_hbm,
    ema_hbm,
    rows_ref,
    slope_ref,
    early_ref,
    weight_ref,
    hidden_buf,
    logits_ref,
    top_ref,
    total_ref,
    peak_ref,
    label_all,
    label_wide,
    stats_ref,
    half_ref,
    part_slots,
    way_slots,
    load_sem,
    fetch_sem,
    label_send,
    label_recv,
    z_send,
    side_send,
    z_recv,
    y_recv,
    x_recv,
    core_recv,
    stat_send,
    part_recv,
    way_recv,
):
    part, way = lax.axis_index("fsdp"), lax.axis_index("vocab")
    own, features = hidden_ref.shape
    count, columns = logits_ref.shape
    length = parts // 2
    z, y = lax.div(part, 2), lax.rem(part, 2)
    x, core = lax.div(way, 2), lax.rem(way, 2)
    low = jnp.minimum(z, length - 1 - z)
    share = own // 3 // 16 * 16
    wide = own - share
    half = features // 2
    piece = half // PIECES
    block = columns // PIECES
    group = 2 * own

    barrier = pltpu.get_barrier_semaphore()
    for step in range(1, parts):
        pl.semaphore_signal(barrier, inc=1, device_id=(way, lax.rem(part + step, parts)), device_id_type=MESH)
    for step in range(1, ways):
        pl.semaphore_signal(barrier, inc=1, device_id=(lax.rem(way + step, ways), part), device_id_type=MESH)

    load = pltpu.make_async_copy(hidden_ref, hidden_buf, load_sem)
    load.start()
    weight_load = pltpu.make_async_copy(weight_hbm, weight_ref, fetch_sem.at[0])
    weight_load.start()
    early_load = pltpu.make_async_copy(ema_hbm.at[pl.ds(0, early_ref.shape[0]), :], early_ref, fetch_sem.at[1])
    early_load.start()
    top_ref[...] = jnp.full_like(top_ref, -jnp.inf)
    total_ref[...] = jnp.zeros_like(total_ref)
    load.wait()

    @pl.loop(0, own // 16)
    def _(index):
        some = pl.ds(pl.multiple_of(index * 16, 16), 16)
        state = hidden_buf[some, :].astype(jnp.float32)
        factor = lax.rsqrt(jnp.mean(state * state, axis=-1, keepdims=True) + EPS)
        rows_ref[pl.ds(pl.multiple_of(part * own + index * 16, 16), 16), :] = (
            state * factor * gain_ref[...].astype(jnp.float32)
        ).astype(jnp.bfloat16)

    pl.semaphore_wait(barrier, parts + ways - 2)

    def source(step):
        both = (step <= 2 * low).astype(jnp.int32)
        left = both * lax.rem(step, 2) + (1 - both) * (2 * z > length - 1).astype(jnp.int32)
        far = both * lax.div(step + 1, 2) + (1 - both) * (step - low)
        return z + far - 2 * far * left, left

    def view(index, start, size, side, s):
        return rows_ref.at[
            pl.ds(pl.multiple_of(index * own + start, 16), size),
            pl.ds(pl.multiple_of(side * half + s * piece, LANES), piece),
        ]

    def send(target, send_sem, recv_sem, device):
        pltpu.make_async_remote_copy(
            src_ref=target, dst_ref=target, send_sem=send_sem, recv_sem=recv_sem, device_id=device, device_id_type=MESH
        ).start()

    across_y = (way, 2 * z + 1 - y)
    across_x = (2 * (1 - x) + core, part)
    across_core = (2 * x + 1 - core, part)

    def arrive(target, recv_sem):
        pltpu.make_async_remote_copy(
            src_ref=target, dst_ref=target, send_sem=side_send.at[0], recv_sem=recv_sem, device_id=across_y, device_id_type=MESH
        ).wait_recv()

    def sent(target, send_sem):
        pltpu.make_async_remote_copy(
            src_ref=target, dst_ref=target, send_sem=send_sem, recv_sem=core_recv.at[0], device_id=across_y, device_id_type=MESH
        ).wait_send()

    def send_z(index, target_z, s, slot):
        where = view(2 * index + y, x * share, wide, core, s)
        send(where, z_send.at[slot], z_recv.at[index, s], (way, 2 * target_z + y))

    def send_y(step, index, s):
        send(view(2 * index + y, x * share, wide, core, s), side_send.at[0], y_recv.at[step, s], across_y)

    def send_x(index, s):
        if share:
            send(view(index, x * wide, share, core, s), side_send.at[1], x_recv.at[index, s], across_x)

    def send_core(index, step, start, size, s):
        send(view(index, start, size, core, s), side_send.at[2], core_recv.at[step], across_core)

    for s in range(PIECES):
        send_y(0, z, s)

        @pl.when(z > 0)
        def _():
            send_z(z, z - 1, s, 0)

        @pl.when(z < length - 1)
        def _():
            send_z(z, z + 1, s, 1)

    labels = []
    for step in range(1, parts):
        labels.append(
            pltpu.make_async_remote_copy(
                src_ref=label_ref,
                dst_ref=label_all.at[part],
                send_sem=label_send.at[step - 1],
                recv_sem=label_recv.at[step - 1],
                device_id=(way, lax.rem(part + step, parts)),
                device_id_type=MESH,
            )
        )
        labels[-1].start()
    label_all[part] = label_ref[...]
    weight_load.wait()

    def group_source(step):
        first = (step == 0).astype(jnp.int32)
        return first * z + (1 - first) * source(step)[0]

    @pl.loop(0, length * PIECES + PIECES + LAG)
    def _(q):
        step, s = lax.div(q, PIECES), lax.rem(q, PIECES)

        @pl.when(q < length * PIECES)
        def _():
            index = 2 * group_source(step) + 1 - y
            arrive(view(index, x * share, wide, core, s), y_recv.at[step, s])
            send_x(index, s)
            send_core(index, step, x * share, wide, s)

        @pl.when(q < (length - 1) * PIECES)
        def _():
            origin, left = source(step + 1)
            onward = z - 1 + 2 * left
            index = 2 * origin + y
            arrive(view(index, x * share, wide, core, s), z_recv.at[origin, s])

            @pl.when(jnp.logical_and(onward >= 0, onward < length))
            def _():
                send_z(origin, onward, s, step + 2)

            send_y(step + 1, origin, s)
            send_x(index, s)
            send_core(index, step + 1, x * share, wide, s)

        if share:
            late = q - LAG
            late_step, late_s = lax.div(late, PIECES), lax.rem(late, PIECES)

            @pl.when(jnp.logical_and(late >= 0, late < length * PIECES))
            def _():
                index = 2 * group_source(late_step) + 1 - y
                arrive(view(index, (1 - x) * wide, share, core, late_s), x_recv.at[index, late_s])
                send_core(index, late_step, (1 - x) * wide, share, late_s)

            @pl.when(jnp.logical_and(late >= 0, late < (length - 1) * PIECES))
            def _():
                index = 2 * source(late_step + 1)[0] + y
                arrive(view(index, (1 - x) * wide, share, core, late_s), x_recv.at[index, late_s])
                send_core(index, late_step + 1, (1 - x) * wide, share, late_s)

        ready = q - PIECES - LAG
        turn, n = lax.div(ready, PIECES), lax.rem(ready, PIECES)

        @pl.when(ready >= 0)
        def _():
            origin = group_source(turn)

            @pl.when(ready == 0)
            def _():
                arrive(rows_ref.at[pl.ds(0, own), pl.ds(0, half)], core_recv.at[0])

            @pl.when(jnp.logical_and(ready > 0, n == 0))
            def _():
                arrive(rows_ref.at[pl.ds(0, group), pl.ds(0, half)], core_recv.at[turn])

            some = pl.ds(pl.multiple_of(origin * group, 16), group)
            result = jnp.dot(
                rows_ref[some, :],
                weight_ref[:, pl.ds(pl.multiple_of(n * block, LANES), block)],
                preferred_element_type=jnp.float32,
            )
            logits_ref[some, pl.ds(pl.multiple_of(n * block, LANES), block)] = result
            pieces = [result[:, start : start + LANES] for start in range(0, block, LANES)]
            old = top_ref[some, :]
            top = functools.reduce(jnp.maximum, pieces, old)
            total_ref[some, :] = total_ref[some, :] * jnp.exp(old - top) + sum(jnp.exp(item - top) for item in pieces)
            top_ref[some, :] = top

    wide_top = top_ref[...].T
    row_top = jnp.max(wide_top, axis=0, keepdims=True)
    row_total = jnp.sum(total_ref[...].T * jnp.exp(wide_top - row_top), axis=0, keepdims=True)
    stats_ref[...] = jnp.concatenate([row_top, row_total], axis=0)

    def combine(terms):
        top = functools.reduce(jnp.maximum, [term[0:1] for term in terms])
        total = sum(term[1:2] * jnp.exp(term[0:1] - top) for term in terms)
        return jnp.concatenate([top, total], axis=0)

    copies = []
    for step in range(1, parts):
        copies.append(
            pltpu.make_async_remote_copy(
                src_ref=stats_ref,
                dst_ref=part_slots.at[part],
                send_sem=stat_send.at[step - 1],
                recv_sem=part_recv.at[step - 1],
                device_id=(way, lax.rem(part + step, parts)),
                device_id_type=MESH,
            )
        )
        copies[-1].start()
    part_slots[part] = stats_ref[...]

    for step in range(1, parts):
        pltpu.make_async_remote_copy(
            src_ref=label_ref,
            dst_ref=label_all.at[lax.rem(part + parts - step, parts)],
            send_sem=label_send.at[step - 1],
            recv_sem=label_recv.at[step - 1],
            device_id=(way, lax.rem(part + step, parts)),
            device_id_type=MESH,
        ).wait_recv()

    @pl.loop(0, parts)
    def _(index):
        some = pl.ds(pl.multiple_of(index * own, 16), own)
        peak = jnp.broadcast_to(jnp.max(top_ref[some, :], axis=1, keepdims=True), (own, LANES))
        first = (way * parts + part) * columns
        label_wide[some, :] = jnp.broadcast_to(label_all[index].astype(jnp.float32), (LANES, own)).T.astype(jnp.int32) - first
        for start in range(0, columns, LANES):
            logits_ref[some, start : start + LANES] = jnp.exp(logits_ref[some, start : start + LANES] - peak)

    for step in range(1, parts):
        pltpu.make_async_remote_copy(
            src_ref=stats_ref,
            dst_ref=part_slots.at[lax.rem(part + parts - step, parts)],
            send_sem=stat_send.at[step - 1],
            recv_sem=part_recv.at[step - 1],
            device_id=(way, lax.rem(part + step, parts)),
            device_id_type=MESH,
        ).wait_recv()
    half_ref[...] = combine([part_slots[index] for index in range(parts)])
    for step in range(1, ways):
        copies.append(
            pltpu.make_async_remote_copy(
                src_ref=half_ref,
                dst_ref=way_slots.at[way],
                send_sem=stat_send.at[parts - 2 + step],
                recv_sem=way_recv.at[step - 1],
                device_id=(lax.rem(way + step, ways), part),
                device_id_type=MESH,
            )
        )
        copies[-1].start()
    way_slots[way] = half_ref[...]
    for step in range(1, ways):
        pltpu.make_async_remote_copy(
            src_ref=half_ref,
            dst_ref=way_slots.at[lax.rem(way + ways - step, ways)],
            send_sem=stat_send.at[parts - 2 + step],
            recv_sem=way_recv.at[step - 1],
            device_id=(lax.rem(way + step, ways), part),
            device_id_type=MESH,
        ).wait_recv()
    final = combine([way_slots[index] for index in range(ways)])
    coefficient = jnp.exp(stats_ref[0:1] - final[0:1]) / final[1:2]
    peak_ref[...] = jnp.broadcast_to(coefficient, (LANES, count)).T

    @pl.loop(0, parts)
    def _(index):
        some = pl.ds(pl.multiple_of(index * own, 16), own)
        scale, label = peak_ref[some, :], label_wide[some, :]
        lane = lax.broadcasted_iota(jnp.int32, (own, LANES), 1)
        for start in range(0, columns, LANES):
            chances = logits_ref[some, start : start + LANES] * scale
            hits = (label == lane + start).astype(jnp.float32)
            slope_ref[some, start : start + LANES] = (chances - hits).astype(slope_ref.dtype)

    for copy in labels + copies:
        copy.wait_send()
    sent(rows_ref.at[pl.ds(0, length * wide), pl.ds(0, half)], side_send.at[0])
    if share:
        sent(rows_ref.at[pl.ds(0, (parts - 1) * share), pl.ds(0, half)], side_send.at[1])
    sent(rows_ref.at[pl.ds(0, (parts - 1) * own), pl.ds(0, half)], side_send.at[2])
    part_view = rows_ref.at[pl.ds(0, wide), pl.ds(0, half)]

    @pl.when(z > 0)
    def _():
        sent(part_view, z_send.at[0])

    @pl.when(z < length - 1)
    def _():
        sent(part_view, z_send.at[1])

    for step in range(1, length):
        onward = z - 1 + 2 * source(step)[1]

        @pl.when(jnp.logical_and(onward >= 0, onward < length))
        def _():
            sent(part_view, z_send.at[step + 1])

    early_load.wait()


def forward(hidden, gain, labels, head_weight, head_ema, parts, ways, early, limit):
    own, features = hidden.shape
    columns = head_weight.shape[1]
    count = own * parts
    length = parts // 2
    anywhere = pl.BlockSpec(memory_space=pl.ANY)
    near = pl.BlockSpec(memory_space=pltpu.VMEM)
    dma = pltpu.SemaphoreType.DMA
    wide = pltpu.VMEM((count, LANES), jnp.float32)
    return pl.pallas_call(
        functools.partial(forward_kernel, parts, ways),
        out_shape=(
            pltpu.VMEM((count, features), jnp.bfloat16),
            pltpu.VMEM((count, columns), jnp.bfloat16),
            pltpu.VMEM((early, columns), jnp.float32),
        ),
        in_specs=[anywhere, near, near, anywhere, anywhere],
        out_specs=(near,) * 3,
        scratch_shapes=[
            pltpu.VMEM((features, columns), jnp.bfloat16),
            pltpu.VMEM((own, features), jnp.bfloat16),
            pltpu.VMEM((count, columns), jnp.float32),
            wide,
            wide,
            wide,
            pltpu.VMEM((parts, 1, own), jnp.int32),
            pltpu.VMEM((count, LANES), jnp.int32),
            pltpu.VMEM((2, count), jnp.float32),
            pltpu.VMEM((2, count), jnp.float32),
            pltpu.VMEM((parts, 2, count), jnp.float32),
            pltpu.VMEM((ways, 2, count), jnp.float32),
            dma,
            dma((2,)),
            dma((parts - 1,)),
            dma((parts - 1,)),
            dma((length + 1,)),
            dma((3,)),
            dma((length, PIECES)),
            dma((length, PIECES)),
            dma((parts, PIECES)),
            dma((length,)),
            dma((parts + ways - 2,)),
            dma((parts - 1,)),
            dma((ways - 1,)),
        ],
        compiler_params=pltpu.CompilerParams(collective_id=0, has_side_effects=True, vmem_limit_bytes=limit),
        name="forward",
    )(hidden, gain, labels, head_weight, head_ema)


def update_kernel(
    tile,
    close,
    rows_ref,
    slope_ref,
    early_ref,
    weight_hbm,
    ema_hbm,
    new_hbm,
    gain_ref,
    rows_buf,
    weight_buf,
    ema_buf,
    new_buf,
    rows_sem,
    weight_sem,
    in_sem,
    out_sem,
):
    count, columns = slope_ref.shape
    features = rows_ref.shape[1]
    tiles, early = features // tile, early_ref.shape[0] // tile
    mix = (1.0 - BETA) / count
    width = min(512, columns)

    def rows_of(index):
        return pl.ds(pl.multiple_of(index * tile, tile), tile)

    def fetch(index):
        slot = lax.rem(index, 2)
        return pltpu.make_async_copy(ema_hbm.at[rows_of(index), :], ema_buf.at[slot], in_sem.at[slot])

    def fetch_rows(index):
        slot = lax.rem(index, 2)
        return pltpu.make_async_copy(rows_ref.at[:, rows_of(index)], rows_buf.at[slot], rows_sem.at[slot])

    def fetch_weight(index):
        slot = lax.rem(index, 2)
        return pltpu.make_async_copy(weight_hbm.at[rows_of(index), :], weight_buf.at[slot], weight_sem.at[slot])

    def store(index):
        slot = lax.rem(index, 2)
        return pltpu.make_async_copy(new_buf.at[slot], new_hbm.at[rows_of(index), :], out_sem.at[slot])

    def work(index, old):
        slot = lax.rem(index, 2)

        @pl.when(index >= 2)
        def _():
            store(index - 2).wait()

        fetch_weight(index).wait()
        if close:
            tall = rows_ref[:, rows_of(index)].T
        else:
            fetch_rows(index).wait()
            tall = rows_buf[slot].T
        total = jnp.zeros((tile, LANES), jnp.float32)
        for start in range(0, columns, width):
            gradient = jnp.dot(tall, slope_ref[:, start : start + width], preferred_element_type=jnp.float32)
            new_buf[slot, :, start : start + width] = BETA * old(start) + mix * gradient * gradient
            product = weight_buf[slot, :, start : start + width].astype(jnp.float32) * gradient
            for lane in range(0, width, LANES):
                total = total + product[:, lane : lane + LANES]
        gain_ref[:, rows_of(index)] = jnp.sum(total.T, axis=0, keepdims=True)
        store(index).start()

        @pl.when(index + 2 < tiles)
        def _():
            fetch_weight(index + 2).start()
            if not close:
                fetch_rows(index + 2).start()

    for index in range(min(2, tiles)):
        fetch_weight(index).start()
        if not close:
            fetch_rows(index).start()
    for index in range(early, min(early + 2, tiles)):
        fetch(index).start()

    @pl.loop(0, early)
    def _(index):
        work(index, lambda start: early_ref[rows_of(index), start : start + width])

    @pl.loop(early, tiles)
    def _(index):
        fetch(index).wait()
        work(index, lambda start: ema_buf[lax.rem(index, 2), :, start : start + width])

        @pl.when(index + 2 < tiles)
        def _():
            fetch(index + 2).start()

    for index in range(max(tiles - 2, 0), tiles):
        store(index).wait()


def head_update(rows, slope, early, head_weight, head_ema, tile, close, limit):
    features, columns = head_ema.shape
    anywhere = pl.BlockSpec(memory_space=pl.ANY)
    near = pl.BlockSpec(memory_space=pltpu.VMEM)
    dma = pltpu.SemaphoreType.DMA
    return pl.pallas_call(
        functools.partial(update_kernel, tile, close),
        out_shape=(
            jax.ShapeDtypeStruct((features, columns), jnp.float32),
            jax.ShapeDtypeStruct((1, features), jnp.float32),
        ),
        in_specs=[near if close else anywhere, near, near, anywhere, anywhere],
        out_specs=(anywhere, near),
        scratch_shapes=[
            pltpu.VMEM((2, 16, LANES) if close else (2, rows.shape[0], tile), jnp.bfloat16),
            pltpu.VMEM((2, tile, columns), jnp.bfloat16),
            pltpu.VMEM((2, tile, columns), jnp.float32),
            pltpu.VMEM((2, tile, columns), jnp.float32),
        ]
        + [dma((2,))] * 4,
        compiler_params=pltpu.CompilerParams(vmem_limit_bytes=limit),
        name="head_update",
    )(rows, slope, early, head_weight, head_ema)


def exchange_kernel(parts, ways, x_ref, y_ref, part_slots, way_slots, half, send_sem, part_sem, way_sem):
    part, way = lax.axis_index("fsdp"), lax.axis_index("vocab")
    barrier = pltpu.get_barrier_semaphore()
    for step in range(1, parts):
        pl.semaphore_signal(barrier, inc=1, device_id=(way, lax.rem(part + step, parts)), device_id_type=MESH)
    for step in range(1, ways):
        pl.semaphore_signal(barrier, inc=1, device_id=(lax.rem(way + step, ways), part), device_id_type=MESH)
    pl.semaphore_wait(barrier, parts + ways - 2)

    copies = []
    for step in range(1, parts):
        copies.append(
            pltpu.make_async_remote_copy(
                src_ref=x_ref,
                dst_ref=part_slots.at[part],
                send_sem=send_sem.at[step - 1],
                recv_sem=part_sem.at[step - 1],
                device_id=(way, lax.rem(part + step, parts)),
                device_id_type=MESH,
            )
        )
        copies[-1].start()
    part_slots[part] = x_ref[...]
    for step in range(1, parts):
        pltpu.make_async_remote_copy(
            src_ref=x_ref,
            dst_ref=part_slots.at[lax.rem(part + parts - step, parts)],
            send_sem=send_sem.at[step - 1],
            recv_sem=part_sem.at[step - 1],
            device_id=(way, lax.rem(part + step, parts)),
            device_id_type=MESH,
        ).wait_recv()
    half[...] = sum(part_slots[index] for index in range(parts))
    for step in range(1, ways):
        copies.append(
            pltpu.make_async_remote_copy(
                src_ref=half,
                dst_ref=way_slots.at[way],
                send_sem=send_sem.at[parts - 2 + step],
                recv_sem=way_sem.at[step - 1],
                device_id=(lax.rem(way + step, ways), part),
                device_id_type=MESH,
            )
        )
        copies[-1].start()
    way_slots[way] = half[...]
    for step in range(1, ways):
        pltpu.make_async_remote_copy(
            src_ref=half,
            dst_ref=way_slots.at[lax.rem(way + ways - step, ways)],
            send_sem=send_sem.at[parts - 2 + step],
            recv_sem=way_sem.at[step - 1],
            device_id=(lax.rem(way + step, ways), part),
            device_id_type=MESH,
        ).wait_recv()
    y_ref[...] = sum(way_slots[index] for index in range(ways))
    for copy in copies:
        copy.wait_send()


def exchange(x, parts, ways):
    return pl.pallas_call(
        functools.partial(exchange_kernel, parts, ways),
        out_shape=jax.ShapeDtypeStruct(x.shape, x.dtype),
        in_specs=[pl.BlockSpec(memory_space=pltpu.VMEM)],
        out_specs=pl.BlockSpec(memory_space=pltpu.VMEM),
        scratch_shapes=[
            pltpu.VMEM((parts,) + x.shape, x.dtype),
            pltpu.VMEM((ways,) + x.shape, x.dtype),
            pltpu.VMEM(x.shape, x.dtype),
            pltpu.SemaphoreType.DMA((parts + ways - 2,)),
            pltpu.SemaphoreType.DMA((parts - 1,)),
            pltpu.SemaphoreType.DMA((ways - 1,)),
        ],
        compiler_params=pltpu.CompilerParams(collective_id=1, has_side_effects=True, vmem_limit_bytes=8 * MIB),
        name="exchange_gain",
    )(x)


def on_device(parts, ways, hidden, norm_gain, labels, head_weight, head_ema, gain_ema):
    batches, own_rows, features = hidden.shape
    own = batches * own_rows
    count = own * parts
    columns = head_weight.shape[1]
    tile = 512 if features % 512 == 0 else 256
    slab = tile * columns * 4
    close = count * features * 2 <= 12 * MIB
    limit = max(features * columns * 2 + count * (columns + 4 * LANES) * 4, 5 * slab) + 4 * MIB
    room = 52 * MIB - limit - count * (features + columns) * 2
    early = min(max(room // slab, 1), features // tile) * tile
    rows, slope, early_ema = forward(
        hidden.reshape(own, features), norm_gain.reshape(1, features), labels.reshape(1, own), head_weight, head_ema, parts, ways, early, limit
    )
    head_new, partial_sum = head_update(rows, slope, early_ema, head_weight, head_ema, tile, close, limit)
    gain_grad = exchange(partial_sum, parts, ways).reshape(features) / norm_gain.astype(jnp.float32)
    gain_new = BETA * gain_ema + (1.0 - BETA) * gain_grad * gain_grad / count
    return (head_new, gain_new)


def solution(mesh):
    return jax.shard_map(
        functools.partial(on_device, mesh.shape["fsdp"], mesh.shape["vocab"]),
        mesh=mesh,
        in_specs=(
            P(None, "fsdp", None),
            P(),
            P(None, "fsdp"),
            P(None, ("vocab", "fsdp")),
            P(None, ("vocab", "fsdp")),
            P(),
        ),
        out_specs=(P(None, ("vocab", "fsdp")), P()),
        check_vma=False,
    )
```

```python
import functools

import jax
import jax.numpy as jnp
from jax import lax
from jax.experimental import pallas as pl
from jax.experimental.pallas import tpu as pltpu
from jax.sharding import PartitionSpec as P

BETA = 0.99
EPS = 1e-05
LANES = 128
PIECES = 4
LAG = 3
MESH = pl.DeviceIdType.MESH
MIB = 1024 * 1024


def forward_kernel(
    parts,
    ways,
    early,
    hidden_ref,
    gain_ref,
    label_ref,
    weight_hbm,
    ema_hbm,
    *refs,
):
    rows_ref, slope_ref = refs[:2]
    weight_refs, early_refs = refs[2 : 2 + PIECES], refs[2 + PIECES : 2 + PIECES + early]
    scratch = refs[2 + PIECES + early :]
    forward_body(
        parts, ways, hidden_ref, gain_ref, label_ref, weight_hbm, ema_hbm, rows_ref, slope_ref, weight_refs, early_refs, *scratch
    )


def forward_body(
    parts,
    ways,
    hidden_ref,
    gain_ref,
    label_ref,
    weight_hbm,
    ema_hbm,
    rows_ref,
    slope_ref,
    weight_refs,
    early_refs,
    logits_ref,
    top_ref,
    total_ref,
    peak_ref,
    label_all,
    label_wide,
    stats_ref,
    half_ref,
    part_slots,
    way_slots,
    fetch_sem,
    label_send,
    label_recv,
    z_send,
    side_send,
    z_recv,
    y_recv,
    x_recv,
    core_recv,
    stat_send,
    part_recv,
    way_recv,
):
    part, way = lax.axis_index("fsdp"), lax.axis_index("vocab")
    own, features = hidden_ref.shape
    count, columns = logits_ref.shape
    length = parts // 2
    z, y = lax.div(part, 2), lax.rem(part, 2)
    x, core = lax.div(way, 2), lax.rem(way, 2)
    low = jnp.minimum(z, length - 1 - z)
    share = own // 3 // 16 * 16
    wide = own - share
    half = features // 2
    piece = half // PIECES
    block = columns // PIECES
    group = 2 * own

    barrier = pltpu.get_barrier_semaphore()
    for step in range(1, parts):
        pl.semaphore_signal(barrier, inc=1, device_id=(way, lax.rem(part + step, parts)), device_id_type=MESH)
    for step in range(1, ways):
        pl.semaphore_signal(barrier, inc=1, device_id=(lax.rem(way + step, ways), part), device_id_type=MESH)

    loads = []
    for n, ref in enumerate(weight_refs):
        loads.append(pltpu.make_async_copy(weight_hbm.at[:, pl.ds(n * block, block)], ref, fetch_sem.at[n]))
    for n, ref in enumerate(early_refs):
        loads.append(pltpu.make_async_copy(ema_hbm.at[pl.ds(n * ref.shape[0], ref.shape[0]), :], ref, fetch_sem.at[PIECES + n]))
    for load in loads:
        load.start()
    top_ref[...] = jnp.full_like(top_ref, -jnp.inf)
    total_ref[...] = jnp.zeros_like(total_ref)

    @pl.loop(0, own // 16)
    def _(index):
        some = pl.ds(pl.multiple_of(index * 16, 16), 16)
        state = hidden_ref[some, :].astype(jnp.float32)
        factor = lax.rsqrt(jnp.mean(state * state, axis=-1, keepdims=True) + EPS)
        rows_ref[pl.ds(pl.multiple_of(part * own + index * 16, 16), 16), :] = (
            state * factor * gain_ref[...].astype(jnp.float32)
        ).astype(jnp.bfloat16)

    pl.semaphore_wait(barrier, parts + ways - 2)

    def source(step):
        both = (step <= 2 * low).astype(jnp.int32)
        left = both * lax.rem(step, 2) + (1 - both) * (2 * z > length - 1).astype(jnp.int32)
        far = both * lax.div(step + 1, 2) + (1 - both) * (step - low)
        return z + far - 2 * far * left, left

    def view(index, start, size, side, s):
        return rows_ref.at[
            pl.ds(pl.multiple_of(index * own + start, 16), size),
            pl.ds(pl.multiple_of(side * half + s * piece, LANES), piece),
        ]

    def send(target, send_sem, recv_sem, device):
        pltpu.make_async_remote_copy(
            src_ref=target, dst_ref=target, send_sem=send_sem, recv_sem=recv_sem, device_id=device, device_id_type=MESH
        ).start()

    across_y = (way, 2 * z + 1 - y)
    across_x = (2 * (1 - x) + core, part)
    across_core = (2 * x + 1 - core, part)

    def arrive(target, recv_sem):
        pltpu.make_async_remote_copy(
            src_ref=target, dst_ref=target, send_sem=side_send.at[0], recv_sem=recv_sem, device_id=across_y, device_id_type=MESH
        ).wait_recv()

    def sent(target, send_sem):
        pltpu.make_async_remote_copy(
            src_ref=target, dst_ref=target, send_sem=send_sem, recv_sem=core_recv.at[0], device_id=across_y, device_id_type=MESH
        ).wait_send()

    def send_z(index, target_z, s, slot):
        where = view(2 * index + y, x * share, wide, core, s)
        send(where, z_send.at[slot], z_recv.at[index, s], (way, 2 * target_z + y))

    def send_y(step, index, s):
        send(view(2 * index + y, x * share, wide, core, s), side_send.at[0], y_recv.at[step, s], across_y)

    def send_x(index, s):
        if share:
            send(view(index, x * wide, share, core, s), side_send.at[1], x_recv.at[index, s], across_x)

    def send_core(index, step, start, size, s):
        send(view(index, start, size, core, s), side_send.at[2], core_recv.at[step], across_core)

    for s in range(PIECES):
        send_y(0, z, s)

        @pl.when(z > 0)
        def _():
            send_z(z, z - 1, s, 0)

        @pl.when(z < length - 1)
        def _():
            send_z(z, z + 1, s, 1)

    labels = []
    for step in range(1, parts):
        labels.append(
            pltpu.make_async_remote_copy(
                src_ref=label_ref,
                dst_ref=label_all.at[part],
                send_sem=label_send.at[step - 1],
                recv_sem=label_recv.at[step - 1],
                device_id=(way, lax.rem(part + step, parts)),
                device_id_type=MESH,
            )
        )
        labels[-1].start()
    label_all[part] = label_ref[...]
    for load in loads[:PIECES]:
        load.wait()

    def group_source(step):
        first = (step == 0).astype(jnp.int32)
        return first * z + (1 - first) * source(step)[0]

    @pl.loop(0, length * PIECES + PIECES + LAG)
    def _(q):
        step, s = lax.div(q, PIECES), lax.rem(q, PIECES)

        @pl.when(q < length * PIECES)
        def _():
            index = 2 * group_source(step) + 1 - y
            arrive(view(index, x * share, wide, core, s), y_recv.at[step, s])
            send_x(index, s)
            send_core(index, step, x * share, wide, s)

        @pl.when(q < (length - 1) * PIECES)
        def _():
            origin, left = source(step + 1)
            onward = z - 1 + 2 * left
            index = 2 * origin + y
            arrive(view(index, x * share, wide, core, s), z_recv.at[origin, s])

            @pl.when(jnp.logical_and(onward >= 0, onward < length))
            def _():
                send_z(origin, onward, s, step + 2)

            send_y(step + 1, origin, s)
            send_x(index, s)
            send_core(index, step + 1, x * share, wide, s)

        if share:
            late = q - LAG
            late_step, late_s = lax.div(late, PIECES), lax.rem(late, PIECES)

            @pl.when(jnp.logical_and(late >= 0, late < length * PIECES))
            def _():
                index = 2 * group_source(late_step) + 1 - y
                arrive(view(index, (1 - x) * wide, share, core, late_s), x_recv.at[index, late_s])
                send_core(index, late_step, (1 - x) * wide, share, late_s)

            @pl.when(jnp.logical_and(late >= 0, late < (length - 1) * PIECES))
            def _():
                index = 2 * source(late_step + 1)[0] + y
                arrive(view(index, (1 - x) * wide, share, core, late_s), x_recv.at[index, late_s])
                send_core(index, late_step + 1, (1 - x) * wide, share, late_s)

        ready = q - PIECES - LAG
        turn, n = lax.div(ready, PIECES), lax.rem(ready, PIECES)

        @pl.when(ready >= 0)
        def _():
            origin = group_source(turn)

            @pl.when(ready == 0)
            def _():
                arrive(rows_ref.at[pl.ds(0, own), pl.ds(0, half)], core_recv.at[0])

            @pl.when(jnp.logical_and(ready > 0, n == 0))
            def _():
                arrive(rows_ref.at[pl.ds(0, group), pl.ds(0, half)], core_recv.at[turn])

            some = pl.ds(pl.multiple_of(origin * group, 16), group)
            for which, weight_ref in enumerate(weight_refs):

                @pl.when(n == which)
                def _():
                    result = jnp.dot(rows_ref[some, :], weight_ref[...], preferred_element_type=jnp.float32)
                    logits_ref[some, which * block : (which + 1) * block] = result
                    pieces = [result[:, start : start + LANES] for start in range(0, block, LANES)]
                    old = top_ref[some, :]
                    top = functools.reduce(jnp.maximum, pieces, old)
                    total_ref[some, :] = total_ref[some, :] * jnp.exp(old - top) + sum(jnp.exp(item - top) for item in pieces)
                    top_ref[some, :] = top

    wide_top = top_ref[...].T
    row_top = jnp.max(wide_top, axis=0, keepdims=True)
    row_total = jnp.sum(total_ref[...].T * jnp.exp(wide_top - row_top), axis=0, keepdims=True)
    stats_ref[...] = jnp.concatenate([row_top, row_total], axis=0)

    def combine(terms):
        top = functools.reduce(jnp.maximum, [term[0:1] for term in terms])
        total = sum(term[1:2] * jnp.exp(term[0:1] - top) for term in terms)
        return jnp.concatenate([top, total], axis=0)

    copies = []
    for step in range(1, parts):
        copies.append(
            pltpu.make_async_remote_copy(
                src_ref=stats_ref,
                dst_ref=part_slots.at[part],
                send_sem=stat_send.at[step - 1],
                recv_sem=part_recv.at[step - 1],
                device_id=(way, lax.rem(part + step, parts)),
                device_id_type=MESH,
            )
        )
        copies[-1].start()
    part_slots[part] = stats_ref[...]

    for step in range(1, parts):
        pltpu.make_async_remote_copy(
            src_ref=label_ref,
            dst_ref=label_all.at[lax.rem(part + parts - step, parts)],
            send_sem=label_send.at[step - 1],
            recv_sem=label_recv.at[step - 1],
            device_id=(way, lax.rem(part + step, parts)),
            device_id_type=MESH,
        ).wait_recv()

    @pl.loop(0, parts)
    def _(index):
        some = pl.ds(pl.multiple_of(index * own, 16), own)
        peak = jnp.broadcast_to(jnp.max(top_ref[some, :], axis=1, keepdims=True), (own, LANES))
        first = (way * parts + part) * columns
        for batch, line in enumerate(range(0, own, label_ref.shape[1])):
            row = label_all[index, batch : batch + 1].astype(jnp.float32)
            wide_row = jnp.broadcast_to(row, (LANES, label_ref.shape[1])).T.astype(jnp.int32) - first
            label_wide[pl.ds(pl.multiple_of(index * own + line, 16), label_ref.shape[1]), :] = wide_row
        for start in range(0, columns, LANES):
            logits_ref[some, start : start + LANES] = jnp.exp(logits_ref[some, start : start + LANES] - peak)

    for step in range(1, parts):
        pltpu.make_async_remote_copy(
            src_ref=stats_ref,
            dst_ref=part_slots.at[lax.rem(part + parts - step, parts)],
            send_sem=stat_send.at[step - 1],
            recv_sem=part_recv.at[step - 1],
            device_id=(way, lax.rem(part + step, parts)),
            device_id_type=MESH,
        ).wait_recv()
    half_ref[...] = combine([part_slots[index] for index in range(parts)])
    for step in range(1, ways):
        copies.append(
            pltpu.make_async_remote_copy(
                src_ref=half_ref,
                dst_ref=way_slots.at[way],
                send_sem=stat_send.at[parts - 2 + step],
                recv_sem=way_recv.at[step - 1],
                device_id=(lax.rem(way + step, ways), part),
                device_id_type=MESH,
            )
        )
        copies[-1].start()
    way_slots[way] = half_ref[...]
    for step in range(1, ways):
        pltpu.make_async_remote_copy(
            src_ref=half_ref,
            dst_ref=way_slots.at[lax.rem(way + ways - step, ways)],
            send_sem=stat_send.at[parts - 2 + step],
            recv_sem=way_recv.at[step - 1],
            device_id=(lax.rem(way + step, ways), part),
            device_id_type=MESH,
        ).wait_recv()
    final = combine([way_slots[index] for index in range(ways)])
    coefficient = jnp.exp(stats_ref[0:1] - final[0:1]) / final[1:2]
    peak_ref[...] = jnp.broadcast_to(coefficient, (LANES, count)).T

    @pl.loop(0, parts)
    def _(index):
        some = pl.ds(pl.multiple_of(index * own, 16), own)
        scale, label = peak_ref[some, :], label_wide[some, :]
        lane = lax.broadcasted_iota(jnp.int32, (own, LANES), 1)
        for start in range(0, columns, LANES):
            chances = logits_ref[some, start : start + LANES] * scale
            hits = (label == lane + start).astype(jnp.float32)
            slope_ref[some, start : start + LANES] = (chances - hits).astype(slope_ref.dtype)

    for copy in labels + copies:
        copy.wait_send()
    sent(rows_ref.at[pl.ds(0, length * wide), pl.ds(0, half)], side_send.at[0])
    if share:
        sent(rows_ref.at[pl.ds(0, (parts - 1) * share), pl.ds(0, half)], side_send.at[1])
    sent(rows_ref.at[pl.ds(0, (parts - 1) * own), pl.ds(0, half)], side_send.at[2])
    part_view = rows_ref.at[pl.ds(0, wide), pl.ds(0, half)]

    @pl.when(z > 0)
    def _():
        sent(part_view, z_send.at[0])

    @pl.when(z < length - 1)
    def _():
        sent(part_view, z_send.at[1])

    for step in range(1, length):
        onward = z - 1 + 2 * source(step)[1]

        @pl.when(jnp.logical_and(onward >= 0, onward < length))
        def _():
            sent(part_view, z_send.at[step + 1])

    for load in loads[PIECES:]:
        load.wait()


def forward(hidden, gain, labels, head_weight, head_ema, parts, ways, early, tile, limit):
    own, features = hidden.shape
    columns = head_weight.shape[1]
    count = own * parts
    length = parts // 2
    anywhere = pl.BlockSpec(memory_space=pl.ANY)
    near = pl.BlockSpec(memory_space=pltpu.VMEM)
    dma = pltpu.SemaphoreType.DMA
    wide = pltpu.VMEM((count, LANES), jnp.float32)
    return pl.pallas_call(
        functools.partial(forward_kernel, parts, ways, early),
        out_shape=(
            pltpu.VMEM((count, features), jnp.bfloat16),
            pltpu.VMEM((count, columns), jnp.bfloat16),
        )
        + (pltpu.VMEM((features, columns // PIECES), jnp.bfloat16),) * PIECES
        + (pltpu.VMEM((tile, columns), jnp.float32),) * early,
        in_specs=[near, near, near, anywhere, anywhere],
        out_specs=(near,) * (2 + PIECES + early),
        scratch_shapes=[
            pltpu.VMEM((count, columns), jnp.float32),
            wide,
            wide,
            wide,
            pltpu.VMEM((parts,) + labels.shape, jnp.int32),
            pltpu.VMEM((count, LANES), jnp.int32),
            pltpu.VMEM((2, count), jnp.float32),
            pltpu.VMEM((2, count), jnp.float32),
            pltpu.VMEM((parts, 2, count), jnp.float32),
            pltpu.VMEM((ways, 2, count), jnp.float32),
            dma((PIECES + early,)),
            dma((parts - 1,)),
            dma((parts - 1,)),
            dma((length + 1,)),
            dma((3,)),
            dma((length, PIECES)),
            dma((length, PIECES)),
            dma((parts, PIECES)),
            dma((length,)),
            dma((parts + ways - 2,)),
            dma((parts - 1,)),
            dma((ways - 1,)),
        ],
        compiler_params=pltpu.CompilerParams(collective_id=0, has_side_effects=True, vmem_limit_bytes=limit),
        name="forward",
    )(hidden, gain, labels, head_weight, head_ema)


def update_kernel(tile, close, early, ema_hbm, rows_ref, slope_ref, *refs):
    weight_refs, early_refs = refs[:PIECES], refs[PIECES : PIECES + early]
    new_hbm, gain_ref, rows_buf, slab, rows_sem, in_sem, out_sem = refs[PIECES + early :]
    count, columns = slope_ref.shape
    tiles = gain_ref.shape[1] // tile
    depth = slab.shape[0]
    mix = (1.0 - BETA) / count
    width = columns // PIECES
    late = list(range(early, tiles))
    order = []
    for index in range(early):
        order += [index] + late[:1]
        late = late[1:]
    order += late

    def fetch(place):
        slot = place % depth
        return pltpu.make_async_copy(ema_hbm.at[pl.ds(order[place] * tile, tile), :], slab.at[slot], in_sem.at[slot])

    def fetch_rows(place):
        return pltpu.make_async_copy(rows_ref.at[:, pl.ds(order[place] * tile, tile)], rows_buf, rows_sem)

    def store(place, start, size):
        slot = place % depth
        return pltpu.make_async_copy(
            slab.at[slot, :, pl.ds(start, size)], new_hbm.at[pl.ds(order[place] * tile, tile), pl.ds(start, size)], out_sem.at[slot]
        )

    if order[0] >= early:
        fetch(0).start()
    for place, index in enumerate(order):
        slot = place % depth
        if place >= depth - 1:
            store(place - depth + 1, 0, columns).wait()
        if place + 1 < tiles and order[place + 1] >= early:
            fetch(place + 1).start()
        if close:
            tall = rows_ref[:, index * tile : (index + 1) * tile].T
        else:
            fetch_rows(place).start()
            fetch_rows(place).wait()
            tall = rows_buf[...].T
        if index >= early:
            fetch(place).wait()
        total = jnp.zeros((tile, LANES), jnp.float32)
        for n, weight_ref in enumerate(weight_refs):
            where = slice(n * width, (n + 1) * width)
            gradient = jnp.dot(tall, slope_ref[:, where], preferred_element_type=jnp.float32)
            old = early_refs[index][:, where] if index < early else slab[slot, :, where]
            slab[slot, :, where] = BETA * old + mix * gradient * gradient
            product = weight_ref[index * tile : (index + 1) * tile, :].astype(jnp.float32) * gradient
            for lane in range(0, width, LANES):
                total = total + product[:, lane : lane + LANES]
            store(place, n * width, width).start()
        gain_ref[:, index * tile : (index + 1) * tile] = jnp.sum(total.T, axis=0, keepdims=True)
    for place in range(max(tiles - depth + 1, 0), tiles):
        store(place, 0, columns).wait()


def head_update(rows, slope, weights, early, head_ema, tile, close, limit):
    features, columns = head_ema.shape
    anywhere = pl.BlockSpec(memory_space=pl.ANY)
    near = pl.BlockSpec(memory_space=pltpu.VMEM)
    dma = pltpu.SemaphoreType.DMA
    return pl.pallas_call(
        functools.partial(update_kernel, tile, close, len(early)),
        out_shape=(
            jax.ShapeDtypeStruct((features, columns), jnp.float32),
            jax.ShapeDtypeStruct((1, features), jnp.float32),
        ),
        in_specs=[anywhere, near if close else anywhere] + [near] * (1 + len(weights) + len(early)),
        out_specs=(anywhere, near),
        scratch_shapes=[
            pltpu.VMEM((16, LANES) if close else (rows.shape[0], tile), jnp.bfloat16),
            pltpu.VMEM((3, tile, columns), jnp.float32),
            dma,
            dma((3,)),
            dma((3,)),
        ],
        compiler_params=pltpu.CompilerParams(vmem_limit_bytes=limit),
        name="head_update",
    )(head_ema, rows, slope, *weights, *early)


def exchange_kernel(parts, ways, x_ref, y_ref, part_slots, way_slots, half, send_sem, part_sem, way_sem):
    part, way = lax.axis_index("fsdp"), lax.axis_index("vocab")
    barrier = pltpu.get_barrier_semaphore()
    for step in range(1, parts):
        pl.semaphore_signal(barrier, inc=1, device_id=(way, lax.rem(part + step, parts)), device_id_type=MESH)
    for step in range(1, ways):
        pl.semaphore_signal(barrier, inc=1, device_id=(lax.rem(way + step, ways), part), device_id_type=MESH)
    pl.semaphore_wait(barrier, parts + ways - 2)

    copies = []
    for step in range(1, parts):
        copies.append(
            pltpu.make_async_remote_copy(
                src_ref=x_ref,
                dst_ref=part_slots.at[part],
                send_sem=send_sem.at[step - 1],
                recv_sem=part_sem.at[step - 1],
                device_id=(way, lax.rem(part + step, parts)),
                device_id_type=MESH,
            )
        )
        copies[-1].start()
    part_slots[part] = x_ref[...]
    for step in range(1, parts):
        pltpu.make_async_remote_copy(
            src_ref=x_ref,
            dst_ref=part_slots.at[lax.rem(part + parts - step, parts)],
            send_sem=send_sem.at[step - 1],
            recv_sem=part_sem.at[step - 1],
            device_id=(way, lax.rem(part + step, parts)),
            device_id_type=MESH,
        ).wait_recv()
    half[...] = sum(part_slots[index] for index in range(parts))
    for step in range(1, ways):
        copies.append(
            pltpu.make_async_remote_copy(
                src_ref=half,
                dst_ref=way_slots.at[way],
                send_sem=send_sem.at[parts - 2 + step],
                recv_sem=way_sem.at[step - 1],
                device_id=(lax.rem(way + step, ways), part),
                device_id_type=MESH,
            )
        )
        copies[-1].start()
    way_slots[way] = half[...]
    for step in range(1, ways):
        pltpu.make_async_remote_copy(
            src_ref=half,
            dst_ref=way_slots.at[lax.rem(way + ways - step, ways)],
            send_sem=send_sem.at[parts - 2 + step],
            recv_sem=way_sem.at[step - 1],
            device_id=(lax.rem(way + step, ways), part),
            device_id_type=MESH,
        ).wait_recv()
    y_ref[...] = sum(way_slots[index] for index in range(ways))
    for copy in copies:
        copy.wait_send()


def exchange(x, parts, ways):
    return pl.pallas_call(
        functools.partial(exchange_kernel, parts, ways),
        out_shape=jax.ShapeDtypeStruct(x.shape, x.dtype),
        in_specs=[pl.BlockSpec(memory_space=pltpu.VMEM)],
        out_specs=pl.BlockSpec(memory_space=pltpu.VMEM),
        scratch_shapes=[
            pltpu.VMEM((parts,) + x.shape, x.dtype),
            pltpu.VMEM((ways,) + x.shape, x.dtype),
            pltpu.VMEM(x.shape, x.dtype),
            pltpu.SemaphoreType.DMA((parts + ways - 2,)),
            pltpu.SemaphoreType.DMA((parts - 1,)),
            pltpu.SemaphoreType.DMA((ways - 1,)),
        ],
        compiler_params=pltpu.CompilerParams(collective_id=1, has_side_effects=True, vmem_limit_bytes=8 * MIB),
        name="exchange_gain",
    )(x)


def on_device(parts, ways, hidden, norm_gain, labels, head_weight, head_ema, gain_ema):
    batches, own_rows, features = hidden.shape
    own = batches * own_rows
    count = own * parts
    columns = head_weight.shape[1]
    tile = 512 if features % 512 == 0 else 256
    slab = tile * columns * 4
    close = count * features * 2 <= 12 * MIB
    limit = max(count * (columns + 4 * LANES) * 4, 3 * slab + (0 if close else count * tile * 2)) + 3 * MIB
    room = 53 * MIB - limit - count * (features + columns) * 2 - features * columns * 2
    early = min(max(room // slab, 0), features // tile)
    rows, slope, *kept = forward(
        hidden.reshape(own, features), norm_gain.reshape(1, features), labels, head_weight, head_ema, parts, ways, early, tile, limit
    )
    head_new, partial_sum = head_update(rows, slope, kept[:PIECES], kept[PIECES:], head_ema, tile, close, limit)
    gain_grad = exchange(partial_sum, parts, ways).reshape(features) / norm_gain.astype(jnp.float32)
    gain_new = BETA * gain_ema + (1.0 - BETA) * gain_grad * gain_grad / count
    return (head_new, gain_new)


def solution(mesh):
    return jax.shard_map(
        functools.partial(on_device, mesh.shape["fsdp"], mesh.shape["vocab"]),
        mesh=mesh,
        in_specs=(
            P(None, "fsdp", None),
            P(),
            P(None, "fsdp"),
            P(None, ("vocab", "fsdp")),
            P(None, ("vocab", "fsdp")),
            P(),
        ),
        out_specs=(P(None, ("vocab", "fsdp")), P()),
        check_vma=False,
    )
```

```python
import functools

import jax
import jax.numpy as jnp
from jax import lax
from jax.experimental import pallas as pl
from jax.experimental.pallas import tpu as pltpu
from jax.sharding import PartitionSpec as P

BETA = 0.99
EPS = 1e-05
LANES = 128
PIECES = 4
LAG = 3
MESH = pl.DeviceIdType.MESH
MIB = 1024 * 1024


def forward_kernel(
    parts,
    ways,
    early,
    hidden_ref,
    gain_ref,
    label_ref,
    weight_hbm,
    ema_hbm,
    *refs,
):
    rows_ref, slope_ref = refs[:2]
    weight_refs, early_refs = refs[2 : 2 + PIECES], refs[2 + PIECES : 2 + PIECES + early]
    scratch = refs[2 + PIECES + early :]
    forward_body(
        parts, ways, hidden_ref, gain_ref, label_ref, weight_hbm, ema_hbm, rows_ref, slope_ref, weight_refs, early_refs, *scratch
    )


def forward_body(
    parts,
    ways,
    hidden_ref,
    gain_ref,
    label_ref,
    weight_hbm,
    ema_hbm,
    rows_ref,
    slope_ref,
    weight_refs,
    early_refs,
    logits_ref,
    top_ref,
    total_ref,
    peak_ref,
    label_all,
    label_wide,
    stats_ref,
    half_ref,
    part_slots,
    way_slots,
    fetch_sem,
    label_send,
    label_recv,
    z_send,
    side_send,
    z_recv,
    y_recv,
    x_recv,
    core_recv,
    stat_send,
    part_recv,
    way_recv,
):
    part, way = lax.axis_index("fsdp"), lax.axis_index("vocab")
    own, features = hidden_ref.shape
    count, columns = logits_ref.shape
    length = parts // 2
    z, y = lax.div(part, 2), lax.rem(part, 2)
    x, core = lax.div(way, 2), lax.rem(way, 2)
    low = jnp.minimum(z, length - 1 - z)
    share = own // 3 // 16 * 16
    wide = own - share
    half = features // 2
    piece = half // PIECES
    block = columns // PIECES
    group = 2 * own

    barrier = pltpu.get_barrier_semaphore()
    for step in range(1, parts):
        pl.semaphore_signal(barrier, inc=1, device_id=(way, lax.rem(part + step, parts)), device_id_type=MESH)
    for step in range(1, ways):
        pl.semaphore_signal(barrier, inc=1, device_id=(lax.rem(way + step, ways), part), device_id_type=MESH)

    loads = []
    for n, ref in enumerate(weight_refs):
        loads.append(pltpu.make_async_copy(weight_hbm.at[:, pl.ds(n * block, block)], ref, fetch_sem.at[n]))
    for n, ref in enumerate(early_refs):
        loads.append(pltpu.make_async_copy(ema_hbm.at[pl.ds(n * ref.shape[0], ref.shape[0]), :], ref, fetch_sem.at[PIECES + n]))
    for load in loads:
        load.start()
    top_ref[...] = jnp.full_like(top_ref, -jnp.inf)
    total_ref[...] = jnp.zeros_like(total_ref)

    @pl.loop(0, own // 16)
    def _(index):
        some = pl.ds(pl.multiple_of(index * 16, 16), 16)
        state = hidden_ref[some, :].astype(jnp.float32)
        factor = lax.rsqrt(jnp.mean(state * state, axis=-1, keepdims=True) + EPS)
        rows_ref[pl.ds(pl.multiple_of(part * own + index * 16, 16), 16), :] = (
            state * factor * gain_ref[...].astype(jnp.float32)
        ).astype(jnp.bfloat16)

    pl.semaphore_wait(barrier, parts + ways - 2)

    def source(step):
        both = (step <= 2 * low).astype(jnp.int32)
        left = both * lax.rem(step, 2) + (1 - both) * (2 * z > length - 1).astype(jnp.int32)
        far = both * lax.div(step + 1, 2) + (1 - both) * (step - low)
        return z + far - 2 * far * left, left

    def view(index, start, size, side, s):
        return rows_ref.at[
            pl.ds(pl.multiple_of(index * own + start, 16), size),
            pl.ds(pl.multiple_of(side * half + s * piece, LANES), piece),
        ]

    def send(target, send_sem, recv_sem, device):
        pltpu.make_async_remote_copy(
            src_ref=target, dst_ref=target, send_sem=send_sem, recv_sem=recv_sem, device_id=device, device_id_type=MESH
        ).start()

    across_y = (way, 2 * z + 1 - y)
    across_x = (2 * (1 - x) + core, part)
    across_core = (2 * x + 1 - core, part)

    def arrive(target, recv_sem):
        pltpu.make_async_remote_copy(
            src_ref=target, dst_ref=target, send_sem=side_send.at[0], recv_sem=recv_sem, device_id=across_y, device_id_type=MESH
        ).wait_recv()

    def sent(target, send_sem):
        pltpu.make_async_remote_copy(
            src_ref=target, dst_ref=target, send_sem=send_sem, recv_sem=core_recv.at[0], device_id=across_y, device_id_type=MESH
        ).wait_send()

    def send_z(index, target_z, s, slot):
        where = view(2 * index + y, x * share, wide, core, s)
        send(where, z_send.at[slot], z_recv.at[index, s], (way, 2 * target_z + y))

    def send_y(step, index, s):
        send(view(2 * index + y, x * share, wide, core, s), side_send.at[0], y_recv.at[step, s], across_y)

    def send_x(index, s):
        if share:
            send(view(index, x * wide, share, core, s), side_send.at[1], x_recv.at[index, s], across_x)

    def send_core(index, step, start, size, s):
        send(view(index, start, size, core, s), side_send.at[2], core_recv.at[step], across_core)

    for s in range(PIECES):
        send_y(0, z, s)

        @pl.when(z > 0)
        def _():
            send_z(z, z - 1, s, 0)

        @pl.when(z < length - 1)
        def _():
            send_z(z, z + 1, s, 1)

    labels = []
    for step in range(1, parts):
        labels.append(
            pltpu.make_async_remote_copy(
                src_ref=label_ref,
                dst_ref=label_all.at[part],
                send_sem=label_send.at[step - 1],
                recv_sem=label_recv.at[step - 1],
                device_id=(way, lax.rem(part + step, parts)),
                device_id_type=MESH,
            )
        )
        labels[-1].start()
    label_all[part] = label_ref[...]
    for load in loads[:PIECES]:
        load.wait()

    def group_source(step):
        first = (step == 0).astype(jnp.int32)
        return first * z + (1 - first) * source(step)[0]

    @pl.loop(0, length * PIECES + PIECES + LAG)
    def _(q):
        step, s = lax.div(q, PIECES), lax.rem(q, PIECES)

        @pl.when(q < length * PIECES)
        def _():
            index = 2 * group_source(step) + 1 - y
            arrive(view(index, x * share, wide, core, s), y_recv.at[step, s])
            send_x(index, s)
            send_core(index, step, x * share, wide, s)

        @pl.when(q < (length - 1) * PIECES)
        def _():
            origin, left = source(step + 1)
            onward = z - 1 + 2 * left
            index = 2 * origin + y
            arrive(view(index, x * share, wide, core, s), z_recv.at[origin, s])

            @pl.when(jnp.logical_and(onward >= 0, onward < length))
            def _():
                send_z(origin, onward, s, step + 2)

            send_y(step + 1, origin, s)
            send_x(index, s)
            send_core(index, step + 1, x * share, wide, s)

        if share:
            late = q - LAG
            late_step, late_s = lax.div(late, PIECES), lax.rem(late, PIECES)

            @pl.when(jnp.logical_and(late >= 0, late < length * PIECES))
            def _():
                index = 2 * group_source(late_step) + 1 - y
                arrive(view(index, (1 - x) * wide, share, core, late_s), x_recv.at[index, late_s])
                send_core(index, late_step, (1 - x) * wide, share, late_s)

            @pl.when(jnp.logical_and(late >= 0, late < (length - 1) * PIECES))
            def _():
                index = 2 * source(late_step + 1)[0] + y
                arrive(view(index, (1 - x) * wide, share, core, late_s), x_recv.at[index, late_s])
                send_core(index, late_step + 1, (1 - x) * wide, share, late_s)

        ready = q - PIECES - LAG
        turn, n = lax.div(ready, PIECES), lax.rem(ready, PIECES)

        @pl.when(ready >= 0)
        def _():
            origin = group_source(turn)

            @pl.when(ready == 0)
            def _():
                arrive(rows_ref.at[pl.ds(0, own), pl.ds(0, half)], core_recv.at[0])

            @pl.when(jnp.logical_and(ready > 0, n == 0))
            def _():
                arrive(rows_ref.at[pl.ds(0, group), pl.ds(0, half)], core_recv.at[turn])

            some = pl.ds(pl.multiple_of(origin * group, 16), group)
            for which, weight_ref in enumerate(weight_refs):

                @pl.when(n == which)
                def _():
                    result = jnp.dot(rows_ref[some, :], weight_ref[...], preferred_element_type=jnp.float32)
                    logits_ref[some, which * block : (which + 1) * block] = result
                    pieces = [result[:, start : start + LANES] for start in range(0, block, LANES)]
                    old = top_ref[some, :]
                    top = functools.reduce(jnp.maximum, pieces, old)
                    total_ref[some, :] = total_ref[some, :] * jnp.exp(old - top) + sum(jnp.exp(item - top) for item in pieces)
                    top_ref[some, :] = top

    wide_top = top_ref[...].T
    row_top = jnp.max(wide_top, axis=0, keepdims=True)
    row_total = jnp.sum(total_ref[...].T * jnp.exp(wide_top - row_top), axis=0, keepdims=True)
    stats_ref[...] = jnp.concatenate([row_top, row_total], axis=0)

    def combine(terms):
        top = functools.reduce(jnp.maximum, [term[0:1] for term in terms])
        total = sum(term[1:2] * jnp.exp(term[0:1] - top) for term in terms)
        return jnp.concatenate([top, total], axis=0)

    copies = []
    for step in range(1, parts):
        copies.append(
            pltpu.make_async_remote_copy(
                src_ref=stats_ref,
                dst_ref=part_slots.at[part],
                send_sem=stat_send.at[step - 1],
                recv_sem=part_recv.at[step - 1],
                device_id=(way, lax.rem(part + step, parts)),
                device_id_type=MESH,
            )
        )
        copies[-1].start()
    part_slots[part] = stats_ref[...]

    for step in range(1, parts):
        pltpu.make_async_remote_copy(
            src_ref=label_ref,
            dst_ref=label_all.at[lax.rem(part + parts - step, parts)],
            send_sem=label_send.at[step - 1],
            recv_sem=label_recv.at[step - 1],
            device_id=(way, lax.rem(part + step, parts)),
            device_id_type=MESH,
        ).wait_recv()

    @pl.loop(0, parts)
    def _(index):
        some = pl.ds(pl.multiple_of(index * own, 16), own)
        peak = jnp.broadcast_to(jnp.max(top_ref[some, :], axis=1, keepdims=True), (own, LANES))
        first = (way * parts + part) * columns
        for batch, line in enumerate(range(0, own, label_ref.shape[1])):
            row = label_all[index, batch : batch + 1].astype(jnp.float32)
            wide_row = jnp.broadcast_to(row, (LANES, label_ref.shape[1])).T.astype(jnp.int32) - first
            label_wide[pl.ds(pl.multiple_of(index * own + line, 16), label_ref.shape[1]), :] = wide_row
        for start in range(0, columns, LANES):
            logits_ref[some, start : start + LANES] = jnp.exp(logits_ref[some, start : start + LANES] - peak)

    for step in range(1, parts):
        pltpu.make_async_remote_copy(
            src_ref=stats_ref,
            dst_ref=part_slots.at[lax.rem(part + parts - step, parts)],
            send_sem=stat_send.at[step - 1],
            recv_sem=part_recv.at[step - 1],
            device_id=(way, lax.rem(part + step, parts)),
            device_id_type=MESH,
        ).wait_recv()
    half_ref[...] = combine([part_slots[index] for index in range(parts)])
    for step in range(1, ways):
        copies.append(
            pltpu.make_async_remote_copy(
                src_ref=half_ref,
                dst_ref=way_slots.at[way],
                send_sem=stat_send.at[parts - 2 + step],
                recv_sem=way_recv.at[step - 1],
                device_id=(lax.rem(way + step, ways), part),
                device_id_type=MESH,
            )
        )
        copies[-1].start()
    way_slots[way] = half_ref[...]
    for step in range(1, ways):
        pltpu.make_async_remote_copy(
            src_ref=half_ref,
            dst_ref=way_slots.at[lax.rem(way + ways - step, ways)],
            send_sem=stat_send.at[parts - 2 + step],
            recv_sem=way_recv.at[step - 1],
            device_id=(lax.rem(way + step, ways), part),
            device_id_type=MESH,
        ).wait_recv()
    final = combine([way_slots[index] for index in range(ways)])
    coefficient = jnp.exp(stats_ref[0:1] - final[0:1]) / final[1:2]
    peak_ref[...] = jnp.broadcast_to(coefficient, (LANES, count)).T

    @pl.loop(0, parts)
    def _(index):
        some = pl.ds(pl.multiple_of(index * own, 16), own)
        scale, label = peak_ref[some, :], label_wide[some, :]
        lane = lax.broadcasted_iota(jnp.int32, (own, LANES), 1)
        for start in range(0, columns, LANES):
            chances = logits_ref[some, start : start + LANES] * scale
            hits = (label == lane + start).astype(jnp.float32)
            slope_ref[some, start : start + LANES] = (chances - hits).astype(slope_ref.dtype)

    for copy in labels + copies:
        copy.wait_send()
    sent(rows_ref.at[pl.ds(0, length * wide), pl.ds(0, half)], side_send.at[0])
    if share:
        sent(rows_ref.at[pl.ds(0, (parts - 1) * share), pl.ds(0, half)], side_send.at[1])
    sent(rows_ref.at[pl.ds(0, (parts - 1) * own), pl.ds(0, half)], side_send.at[2])
    part_view = rows_ref.at[pl.ds(0, wide), pl.ds(0, half)]

    @pl.when(z > 0)
    def _():
        sent(part_view, z_send.at[0])

    @pl.when(z < length - 1)
    def _():
        sent(part_view, z_send.at[1])

    for step in range(1, length):
        onward = z - 1 + 2 * source(step)[1]

        @pl.when(jnp.logical_and(onward >= 0, onward < length))
        def _():
            sent(part_view, z_send.at[step + 1])

    for load in loads[PIECES:]:
        load.wait()


def forward(hidden, gain, labels, head_weight, head_ema, parts, ways, early, tile, limit):
    own, features = hidden.shape
    columns = head_weight.shape[1]
    count = own * parts
    length = parts // 2
    anywhere = pl.BlockSpec(memory_space=pl.ANY)
    near = pl.BlockSpec(memory_space=pltpu.VMEM)
    dma = pltpu.SemaphoreType.DMA
    wide = pltpu.VMEM((count, LANES), jnp.float32)
    return pl.pallas_call(
        functools.partial(forward_kernel, parts, ways, early),
        out_shape=(
            pltpu.VMEM((count, features), jnp.bfloat16),
            pltpu.VMEM((count, columns), jnp.bfloat16),
        )
        + (pltpu.VMEM((features, columns // PIECES), jnp.bfloat16),) * PIECES
        + (pltpu.VMEM((tile, columns), jnp.float32),) * early,
        in_specs=[near, near, near, anywhere, anywhere],
        out_specs=(near,) * (2 + PIECES + early),
        scratch_shapes=[
            pltpu.VMEM((count, columns), jnp.float32),
            wide,
            wide,
            wide,
            pltpu.VMEM((parts,) + labels.shape, jnp.int32),
            pltpu.VMEM((count, LANES), jnp.int32),
            pltpu.VMEM((2, count), jnp.float32),
            pltpu.VMEM((2, count), jnp.float32),
            pltpu.VMEM((parts, 2, count), jnp.float32),
            pltpu.VMEM((ways, 2, count), jnp.float32),
            dma((PIECES + early,)),
            dma((parts - 1,)),
            dma((parts - 1,)),
            dma((length + 1,)),
            dma((3,)),
            dma((length, PIECES)),
            dma((length, PIECES)),
            dma((parts, PIECES)),
            dma((length,)),
            dma((parts + ways - 2,)),
            dma((parts - 1,)),
            dma((ways - 1,)),
        ],
        compiler_params=pltpu.CompilerParams(collective_id=0, has_side_effects=True, vmem_limit_bytes=limit),
        name="forward",
    )(hidden, gain, labels, head_weight, head_ema)


def update_kernel(tile, close, early, ema_hbm, rows_ref, slope_ref, *refs):
    weight_refs, early_refs = refs[:PIECES], refs[PIECES : PIECES + early]
    new_hbm, gain_ref, rows_buf, slab, rows_sem, in_sem, out_sem = refs[PIECES + early :]
    count, columns = slope_ref.shape
    tiles = gain_ref.shape[1] // tile
    depth = slab.shape[0]
    mix = (1.0 - BETA) / count
    width = columns // PIECES
    late = iter(range(early, tiles))
    early_at = {tiles * index // early: index for index in range(early)} if early else {}
    order = [early_at[place] if place in early_at else next(late) for place in range(tiles)]

    def fetch(place):
        slot = place % depth
        return pltpu.make_async_copy(ema_hbm.at[pl.ds(order[place] * tile, tile), :], slab.at[slot], in_sem.at[slot])

    def fetch_rows(place):
        return pltpu.make_async_copy(rows_ref.at[:, pl.ds(order[place] * tile, tile)], rows_buf, rows_sem)

    def store(place, start, size):
        slot = place % depth
        return pltpu.make_async_copy(
            slab.at[slot, :, pl.ds(start, size)], new_hbm.at[pl.ds(order[place] * tile, tile), pl.ds(start, size)], out_sem.at[slot]
        )

    if order[0] >= early:
        fetch(0).start()
    for place, index in enumerate(order):
        slot = place % depth
        if place >= depth - 1:
            store(place - depth + 1, 0, columns).wait()
        if place + 1 < tiles and order[place + 1] >= early:
            fetch(place + 1).start()
        if close:
            tall = rows_ref[:, index * tile : (index + 1) * tile].T
        else:
            fetch_rows(place).start()
            fetch_rows(place).wait()
            tall = rows_buf[...].T
        if index >= early:
            fetch(place).wait()
        total = jnp.zeros((tile, LANES), jnp.float32)
        for n, weight_ref in enumerate(weight_refs):
            where = slice(n * width, (n + 1) * width)
            gradient = jnp.dot(tall, slope_ref[:, where], preferred_element_type=jnp.float32)
            old = early_refs[index][:, where] if index < early else slab[slot, :, where]
            slab[slot, :, where] = BETA * old + mix * gradient * gradient
            product = weight_ref[index * tile : (index + 1) * tile, :].astype(jnp.float32) * gradient
            for lane in range(0, width, LANES):
                total = total + product[:, lane : lane + LANES]
            store(place, n * width, width).start()
        gain_ref[:, index * tile : (index + 1) * tile] = jnp.sum(total.T, axis=0, keepdims=True)
    for place in range(max(tiles - depth + 1, 0), tiles):
        store(place, 0, columns).wait()


def head_update(rows, slope, weights, early, head_ema, tile, close, limit):
    features, columns = head_ema.shape
    anywhere = pl.BlockSpec(memory_space=pl.ANY)
    near = pl.BlockSpec(memory_space=pltpu.VMEM)
    dma = pltpu.SemaphoreType.DMA
    return pl.pallas_call(
        functools.partial(update_kernel, tile, close, len(early)),
        out_shape=(
            jax.ShapeDtypeStruct((features, columns), jnp.float32),
            jax.ShapeDtypeStruct((1, features), jnp.float32),
        ),
        in_specs=[anywhere, near if close else anywhere] + [near] * (1 + len(weights) + len(early)),
        out_specs=(anywhere, near),
        scratch_shapes=[
            pltpu.VMEM((16, LANES) if close else (rows.shape[0], tile), jnp.bfloat16),
            pltpu.VMEM((3, tile, columns), jnp.float32),
            dma,
            dma((3,)),
            dma((3,)),
        ],
        compiler_params=pltpu.CompilerParams(vmem_limit_bytes=limit),
        name="head_update",
    )(head_ema, rows, slope, *weights, *early)


def exchange_kernel(parts, ways, x_ref, y_ref, part_slots, way_slots, half, send_sem, part_sem, way_sem):
    part, way = lax.axis_index("fsdp"), lax.axis_index("vocab")
    barrier = pltpu.get_barrier_semaphore()
    for step in range(1, parts):
        pl.semaphore_signal(barrier, inc=1, device_id=(way, lax.rem(part + step, parts)), device_id_type=MESH)
    for step in range(1, ways):
        pl.semaphore_signal(barrier, inc=1, device_id=(lax.rem(way + step, ways), part), device_id_type=MESH)
    pl.semaphore_wait(barrier, parts + ways - 2)

    copies = []
    for step in range(1, parts):
        copies.append(
            pltpu.make_async_remote_copy(
                src_ref=x_ref,
                dst_ref=part_slots.at[part],
                send_sem=send_sem.at[step - 1],
                recv_sem=part_sem.at[step - 1],
                device_id=(way, lax.rem(part + step, parts)),
                device_id_type=MESH,
            )
        )
        copies[-1].start()
    part_slots[part] = x_ref[...]
    for step in range(1, parts):
        pltpu.make_async_remote_copy(
            src_ref=x_ref,
            dst_ref=part_slots.at[lax.rem(part + parts - step, parts)],
            send_sem=send_sem.at[step - 1],
            recv_sem=part_sem.at[step - 1],
            device_id=(way, lax.rem(part + step, parts)),
            device_id_type=MESH,
        ).wait_recv()
    half[...] = sum(part_slots[index] for index in range(parts))
    for step in range(1, ways):
        copies.append(
            pltpu.make_async_remote_copy(
                src_ref=half,
                dst_ref=way_slots.at[way],
                send_sem=send_sem.at[parts - 2 + step],
                recv_sem=way_sem.at[step - 1],
                device_id=(lax.rem(way + step, ways), part),
                device_id_type=MESH,
            )
        )
        copies[-1].start()
    way_slots[way] = half[...]
    for step in range(1, ways):
        pltpu.make_async_remote_copy(
            src_ref=half,
            dst_ref=way_slots.at[lax.rem(way + ways - step, ways)],
            send_sem=send_sem.at[parts - 2 + step],
            recv_sem=way_sem.at[step - 1],
            device_id=(lax.rem(way + step, ways), part),
            device_id_type=MESH,
        ).wait_recv()
    y_ref[...] = sum(way_slots[index] for index in range(ways))
    for copy in copies:
        copy.wait_send()


def exchange(x, parts, ways):
    return pl.pallas_call(
        functools.partial(exchange_kernel, parts, ways),
        out_shape=jax.ShapeDtypeStruct(x.shape, x.dtype),
        in_specs=[pl.BlockSpec(memory_space=pltpu.VMEM)],
        out_specs=pl.BlockSpec(memory_space=pltpu.VMEM),
        scratch_shapes=[
            pltpu.VMEM((parts,) + x.shape, x.dtype),
            pltpu.VMEM((ways,) + x.shape, x.dtype),
            pltpu.VMEM(x.shape, x.dtype),
            pltpu.SemaphoreType.DMA((parts + ways - 2,)),
            pltpu.SemaphoreType.DMA((parts - 1,)),
            pltpu.SemaphoreType.DMA((ways - 1,)),
        ],
        compiler_params=pltpu.CompilerParams(collective_id=1, has_side_effects=True, vmem_limit_bytes=8 * MIB),
        name="exchange_gain",
    )(x)


def on_device(parts, ways, hidden, norm_gain, labels, head_weight, head_ema, gain_ema):
    batches, own_rows, features = hidden.shape
    own = batches * own_rows
    count = own * parts
    columns = head_weight.shape[1]
    tile = 512 if features % 512 == 0 else 256
    slab = tile * columns * 4
    close = count * features * 2 <= 12 * MIB
    limit = max(count * (columns + 4 * LANES) * 4, 3 * slab + (0 if close else count * tile * 2)) + 3 * MIB
    room = 53 * MIB - limit - count * (features + columns) * 2 - features * columns * 2
    early = min(max(room // slab, 0), features // tile)
    rows, slope, *kept = forward(
        hidden.reshape(own, features), norm_gain.reshape(1, features), labels, head_weight, head_ema, parts, ways, early, tile, limit
    )
    head_new, partial_sum = head_update(rows, slope, kept[:PIECES], kept[PIECES:], head_ema, tile, close, limit)
    gain_grad = exchange(partial_sum, parts, ways).reshape(features) / norm_gain.astype(jnp.float32)
    gain_new = BETA * gain_ema + (1.0 - BETA) * gain_grad * gain_grad / count
    return (head_new, gain_new)


def solution(mesh):
    return jax.shard_map(
        functools.partial(on_device, mesh.shape["fsdp"], mesh.shape["vocab"]),
        mesh=mesh,
        in_specs=(
            P(None, "fsdp", None),
            P(),
            P(None, "fsdp"),
            P(None, ("vocab", "fsdp")),
            P(None, ("vocab", "fsdp")),
            P(),
        ),
        out_specs=(P(None, ("vocab", "fsdp")), P()),
        check_vma=False,
    )
```
